1024 devices in a mesh: ctx: 128 (over z, y_lo, core), kvh: 8 (over y_hi, x).
Axes of the slice: x: 4, y: 8 (y_hi: 2, y_lo: 4; y = y_hi * 4 + y_lo), z: 16, core: 2. Of those that a mesh axis runs over, the one named last changes fastest.
Arguments:
- queries: bfloat16 [65536, 32, 128], P('ctx', 'kvh'), may hold values from -128 to 128
- keys_values: bfloat16 [2, 65536, 8, 128], P(None, 'ctx', 'kvh'), may hold values from -6 to 6
- carry_out: float32 [65536, 32, 128], P('ctx', 'kvh'), may hold values from -1.75 to 1.75
- carry_lse: float32 [32, 65536], P('kvh', 'ctx'), may hold values from 6 to 10
Outputs:
- out_state: float32 [65536, 32, 128], P('ctx', 'kvh')
- out_lse: float32 [32, 65536], P('kvh', 'ctx')
The draws below stay inside these ranges and needn't reach their ends.
All inputs are finite; a program needn't handle non-finite values.
Results may differ from the reference program's by a relative error of at most 0.0009.
Values may be sent and summed in bfloat16 or wider, within the bound.
A program may use at most 32 MiB of HBM per device.

```python
import jax
import jax.numpy as jnp
from jax import lax

HQ = 32
KVH = 8
HD = 128
TOK_DEV = 512
WIN = 3
LAG = 64
SEQ = 65536


def shared_draw(key):
    base = jax.random.fold_in(key, 17)
    subkeys = jax.random.split(base, 9)
    key_rows = jnp.clip(jax.random.normal(subkeys[0], (SEQ, KVH, HD), jnp.float32), -4.0, 4.0)
    value_rows = jnp.clip(jax.random.normal(subkeys[2], (SEQ, KVH, HD), jnp.float32), -6.0, 6.0)
    return (key_rows, value_rows, subkeys)


def draw_keys_values(key, part):
    key_rows, value_rows, subkeys = shared_draw(key)
    return jnp.stack([key_rows, value_rows]).astype(jnp.bfloat16)


def draw_queries(key, part):
    key_rows, value_rows, subkeys = shared_draw(key)
    drawn = jnp.clip(jax.random.normal(subkeys[3], (SEQ, HQ, HD), jnp.float32), -6.0, 6.0)
    return drawn.astype(jnp.bfloat16)


def steps_of(stream_key, dims, pieces, least, top_value):
    factor_of, own = 1.0, jax.random.fold_in(stream_key, 6)
    for dim, parts in pieces:
        steps = jnp.exp(jax.random.uniform(jax.random.fold_in(own, dim), (parts,), jnp.float32, least / len(pieces), top_value / len(pieces)))
        factor_of = factor_of * jnp.repeat(steps, dims[dim] // parts).reshape([-1 if axis == dim else 1 for axis in range(len(dims))])
    return factor_of


def normal_values(rng, shape, deviation, bound, shards=(), kind=jnp.bfloat16):
    values = deviation * jax.random.normal(rng, shape, jnp.float32)
    if shards:
        values = values * steps_of(rng, shape, shards, -0.22, 0.18)
    return jnp.clip(values, -bound, bound).astype(kind)


def setup_inputs(seed: int = 0) -> dict:
    key_list = jax.random.split(jax.random.key(seed), 5)
    queries = draw_queries(jax.random.fold_in(key_list[4], 71), 0)
    keys_values = draw_keys_values(jax.random.fold_in(key_list[4], 71), 0)
    carry_out = normal_values(key_list[2], (SEQ, HQ, HD), 0.3, 1.75, ((0, 128), (1, 8)), jnp.float32)
    carry_lse = jnp.clip(6.0 + 4.0 * jax.random.uniform(key_list[3], (HQ, SEQ), jnp.float32) ** steps_of(key_list[3], (HQ, SEQ), ((0, 8), (1, 128)), -0.2, 0.2), 6.0, 10.0)
    return dict(queries=queries, keys_values=keys_values, carry_out=carry_out, carry_lse=carry_lse)


def reference(queries, keys_values, carry_out, carry_lse):
    length = queries.shape[0]
    block_count = length // TOK_DEV
    per_group = HQ // KVH
    scaling = HD ** -0.5
    leading = jnp.zeros((2, WIN * TOK_DEV, KVH, HD), keys_values.dtype)
    padded = jnp.concatenate([leading, keys_values], axis=1)
    columns = jnp.arange(WIN * TOK_DEV, dtype=jnp.int32) // TOK_DEV

    def one_block(block_index):
        start = block_index * TOK_DEV
        query_rows = lax.dynamic_slice_in_dim(queries, start, TOK_DEV, 0).astype(jnp.float32)
        query_rows = query_rows.reshape(TOK_DEV, KVH, per_group, HD)
        kv_start = jnp.maximum(block_index - LAG, 0) * TOK_DEV
        window = lax.dynamic_slice_in_dim(padded, kv_start, WIN * TOK_DEV, 1).astype(jnp.float32)
        usable = (block_index - LAG - WIN + columns) >= 0
        active = block_index - LAG - 1 >= 0
        scores = jnp.einsum("tgrd,kgd->grtk", query_rows, window[0]) * scaling
        scores = jnp.where(usable, scores, -jnp.inf)
        top_score = jnp.where(active, jnp.max(scores, axis=-1), 0.0)
        weights = jnp.exp(scores - top_score[..., None])
        weight_sum = jnp.where(active, jnp.sum(weights, axis=-1), 1.0)
        rounded = lax.optimization_barrier(weights.astype(jnp.bfloat16)).astype(jnp.float32)
        blended = jnp.einsum("grtk,kgd->tgrd", rounded, window[1])
        partial_value = blended / jnp.transpose(weight_sum, (2, 0, 1))[..., None]
        window_lse = top_score + jnp.log(weight_sum)
        lse_before = lax.dynamic_slice_in_dim(carry_lse, start, TOK_DEV, 1).reshape(KVH, per_group, TOK_DEV)
        state_before = lax.dynamic_slice_in_dim(carry_out, start, TOK_DEV, 0).reshape(TOK_DEV, KVH, per_group, HD)
        ceiling = jnp.maximum(lse_before, window_lse)
        merged = ceiling + jnp.log(jnp.exp(lse_before - ceiling) + jnp.exp(window_lse - ceiling))
        result = state_before * jnp.transpose(jnp.exp(lse_before - merged), (2, 0, 1))[..., None]
        result = result + partial_value * jnp.transpose(jnp.exp(window_lse - merged), (2, 0, 1))[..., None]
        result = jnp.where(active, result, state_before)
        merged = jnp.where(active, merged, lse_before)
        return result.reshape(TOK_DEV, HQ, HD), merged.reshape(HQ, TOK_DEV)

    results, merged_all = lax.map(one_block, jnp.arange(block_count, dtype=jnp.int32))
    out_state = results.reshape(length, HQ, HD)
    out_lse = jnp.transpose(merged_all, (1, 0, 2)).reshape(HQ, length)
    return out_state, out_lse
```

```python
import functools
import math

import jax
import jax.numpy as jnp
from jax import lax
from jax.experimental import pallas as pl
from jax.experimental.pallas import tpu as pltpu
from jax.sharding import PartitionSpec as P

MESH = pl.DeviceIdType.MESH
WIN = 3
TILE = 256


def kernel(
    n_ctx, per_group, q_hbm, kv_hbm, carry_hbm, clse_ref, out_hbm, olse_ref,
    q, base, kbuf, vbuf, ibuf, scores, weights, acc, top, total, factor, stat,
    in_sem, out_sem, leg_send, mid_recv, fwd_send, recv, spread_send,
):
    rows = q.shape[0]
    toks = kbuf.shape[1]
    half = toks // 2
    lag = n_ctx // 2
    leg = n_ctx // 4
    n_tiles = rows // TILE
    me = lax.axis_index("ctx")
    kvh = lax.axis_index("kvh")
    core = lax.rem(me, 2)
    upward = jnp.logical_and(me >= leg, me < 3 * leg)
    way = jnp.where(upward, 0, 1)
    passed = jnp.where(upward, me - leg, lax.rem(me + leg, n_ctx))
    is_source = me < lag - 1
    passes = passed < lag - 1
    lands = me >= lag + 2
    final = jnp.minimum(passed + lag + 2, n_ctx - 1)
    final_slot = jnp.where(passed == lag - 2, 2, 1)

    def at(device):
        return (device, kvh)

    barrier = pltpu.get_barrier_semaphore()

    def tell(device):
        pl.semaphore_signal(barrier, inc=1, device_id=at(device), device_id_type=MESH)

    @pl.when(passes)
    def _():
        tell(passed)

    @pl.when(lands)
    def _():
        tell(me - lag - 2 + leg)
        tell(lax.rem(me - lag - 2 - leg + n_ctx, n_ctx))

    @pl.when(me == n_ctx - 1)
    def _():
        tell(lag - 2 + leg)
        tell(lag - 2 - leg)

    @pl.when(me >= lag + 3)
    def _():
        tell(me - 1)

    @pl.when(jnp.logical_and(me >= lag + 1, me < n_ctx - 1))
    def _():
        tell(me + 1)

    peers = (
        2 * is_source.astype(jnp.int32)
        + passes.astype(jnp.int32)
        + lands.astype(jnp.int32)
        + jnp.logical_and(lands, me < n_ctx - 1).astype(jnp.int32)
    )
    pl.semaphore_wait(barrier, peers)

    def leg_copy(kind, w):
        device = me + leg if w == 0 else lax.rem(me - leg + n_ctx, n_ctx)
        return pltpu.make_async_remote_copy(
            src_ref=kv_hbm.at[pl.ds(kind * toks + w * half, half)],
            dst_ref=ibuf.at[kind],
            send_sem=leg_send.at[kind, w],
            recv_sem=mid_recv.at[kind],
            device_id=at(device),
            device_id_type=MESH,
        )

    def pass_copy(kind):
        buf = kbuf if kind == 0 else vbuf
        return pltpu.make_async_remote_copy(
            src_ref=ibuf.at[kind],
            dst_ref=buf.at[final_slot, pl.ds(pl.multiple_of(way * half, half), half)],
            send_sem=fwd_send.at[kind],
            recv_sem=recv.at[final_slot, 2 * kind + way],
            device_id=at(final),
            device_id_type=MESH,
        )

    def piece(kind, slot, w):
        buf = kbuf if kind == 0 else vbuf
        return buf.at[slot, pl.ds(w * half, half)]

    def spread_copy(kind, w, to):
        slot, device = ((2, me - 1), (0, me + 1))[to]
        return pltpu.make_async_remote_copy(
            src_ref=piece(kind, 1, w),
            dst_ref=piece(kind, slot, w),
            send_sem=spread_send.at[to, 2 * kind + w],
            recv_sem=recv.at[slot, 2 * kind + w],
            device_id=at(device),
            device_id_type=MESH,
        )

    def arrived(kind, slot, w):
        pltpu.make_async_remote_copy(
            src_ref=piece(kind, slot, w),
            dst_ref=piece(kind, slot, w),
            send_sem=spread_send.at[0, 2 * kind + w],
            recv_sem=recv.at[slot, 2 * kind + w],
            device_id=at(me),
            device_id_type=MESH,
        ).wait_recv()

    def start_legs(kind):
        @pl.when(is_source)
        def _():
            for w in range(2):
                leg_copy(kind, w).start()

    def pass_on(kind):
        @pl.when(passes)
        def _():
            leg_copy(kind, 0).wait_recv()
            pass_copy(kind).start()

    def land_and_spread(kind):
        @pl.when(lands)
        def _():
            for w in range(2):
                arrived(kind, 1, w)
                spread_copy(kind, w, 0).start()

                @pl.when(me < n_ctx - 1)
                def _():
                    spread_copy(kind, w, 1).start()

    start_legs(0)

    carry_in = pltpu.make_async_copy(carry_hbm, base, in_sem.at[0])
    carry_in.start()
    active = me >= lag + 1
    q_in = pltpu.make_async_copy(q_hbm, q, in_sem.at[1])

    @pl.when(active)
    def _():
        q_in.start()

    def tiles(body):
        def step(i, c):
            body(pl.ds(pl.multiple_of(i * TILE, TILE), TILE))
            return c

        lax.fori_loop(0, n_tiles, step, 0)

    lanes = stat.shape[1]
    lse_rows = rows // per_group

    @pl.when(active)
    def _():
        for h in range(per_group):
            row = clse_ref[pl.ds(h, 1), :]
            stat[pl.ds(h, lse_rows, stride=per_group), :] = jnp.transpose(
                jnp.broadcast_to(row, (lanes, lse_rows))
            )

        def init(t):
            top[t, :] = jnp.full((TILE, lanes), -jnp.inf, jnp.float32)
            total[t, :] = jnp.zeros((TILE, lanes), jnp.float32)
            acc[t, :] = jnp.zeros((TILE, lanes), jnp.float32)

        tiles(init)
        q_in.wait()

    pass_on(0)
    start_legs(1)

    def score_piece(slot, w):
        keys = kbuf[slot, pl.ds(w * half, half), :]

        def tile(t):
            s = lax.dot_general(
                q[t, :], keys, (((1,), (1,)), ((), ())), preferred_element_type=jnp.float32
            )
            scores[slot, w, t, :] = s
            m = top[t, :]
            for c in range(0, half, lanes):
                m = jnp.maximum(m, s[:, c : c + lanes])
            top[t, :] = m

        tiles(tile)

    scale = q.shape[1] ** -0.5
    in_two = scale * math.log2(math.e)

    def weight_piece(slot, w):
        def tile(t):
            m = top[t, :]
            total_tile = total[t, :]
            for c in range(0, half, lanes):
                p = jnp.exp2((scores[slot, w, t, pl.ds(c, lanes)] - m) * in_two)
                total_tile = total_tile + p
                weights[slot, w, t, pl.ds(c, lanes)] = p.astype(jnp.bfloat16)
            total[t, :] = total_tile

        tiles(tile)

    def value_piece(slot, w):
        values = vbuf[slot, pl.ds(w * half, half), :]

        def tile(t):
            acc[t, :] += jnp.dot(
                weights[slot, w, t, :], values, preferred_element_type=jnp.float32
            )

        tiles(tile)

    mate = jnp.where(core == 0, 2, 0)
    other = jnp.where(core == 0, 0, 2)
    has = {
        "mid": (1, lands),
        "mate": (mate, me - lag - WIN + mate >= 0),
        "other": (other, me - lag - WIN + other >= 0),
    }

    def each(name, body, wait_kind=None):
        slot, there = has[name]

        @pl.when(jnp.logical_and(active, there))
        def _():
            for w in range(2):
                if wait_kind is not None:
                    arrived(wait_kind, slot, w)
                body(slot, w)

    land_and_spread(0)
    each("mid", score_piece)
    each("mate", score_piece, 0)
    pass_on(1)
    each("other", score_piece, 0)

    @pl.when(active)
    def _():
        def tile(t):
            top[t, :] = jnp.broadcast_to(
                jnp.max(top[t, :], axis=1, keepdims=True), (TILE, lanes)
            )

        tiles(tile)

    each("mid", weight_piece)
    each("mate", weight_piece)
    each("other", weight_piece)
    carry_in.wait()

    @pl.when(active)
    def _():
        def tile(t):
            weight_sum = jnp.broadcast_to(
                jnp.sum(total[t, :], axis=1, keepdims=True), (TILE, lanes)
            )
            window_lse = top[t, :] * scale + jnp.log(weight_sum)
            before = stat[t, :]
            ceiling = jnp.maximum(before, window_lse)
            merged = ceiling + jnp.log(
                jnp.exp(before - ceiling) + jnp.exp(window_lse - ceiling)
            )
            base[t, :] = base[t, :] * jnp.exp(before - merged)
            factor[t, :] = jnp.exp(window_lse - merged) / weight_sum
            stat[t, :] = merged

        tiles(tile)
        for h in range(per_group):
            olse_ref[pl.ds(h, 1), :] = jnp.transpose(
                stat[pl.ds(h, lse_rows, stride=per_group), :]
            )[0:1, :]

    @pl.when(jnp.logical_not(active))
    def _():
        olse_ref[...] = clse_ref[...]

    land_and_spread(1)
    each("mid", value_piece)
    each("mate", value_piece, 1)
    each("other", value_piece, 1)

    @pl.when(active)
    def _():
        def tile(t):
            base[t, :] = base[t, :] + acc[t, :] * factor[t, :]

        tiles(tile)

    put = pltpu.make_async_copy(base, out_hbm, out_sem)
    put.start()

    @pl.when(is_source)
    def _():
        for kind in range(2):
            for w in range(2):
                leg_copy(kind, w).wait_send()

    @pl.when(passes)
    def _():
        for kind in range(2):
            pass_copy(kind).wait_send()

    @pl.when(lands)
    def _():
        for kind in range(2):
            for w in range(2):
                spread_copy(kind, w, 0).wait_send()

                @pl.when(me < n_ctx - 1)
                def _():
                    spread_copy(kind, w, 1).wait_send()

    put.wait()


def body(n_ctx, queries, keys_values, carry_out, carry_lse):
    toks, heads, width = queries.shape
    kv_local = keys_values.shape[2]
    rows = toks * heads
    half = toks // 2
    vmem, anywhere = pltpu.VMEM, pl.ANY
    out, lse = pl.pallas_call(
        functools.partial(kernel, n_ctx, heads // kv_local),
        name="window_attention",
        out_shape=(
            jax.ShapeDtypeStruct((rows, width), jnp.float32),
            jax.ShapeDtypeStruct(carry_lse.shape, jnp.float32),
        ),
        in_specs=[
            pl.BlockSpec(memory_space=anywhere),
            pl.BlockSpec(memory_space=anywhere),
            pl.BlockSpec(memory_space=anywhere),
            pl.BlockSpec(memory_space=vmem),
        ],
        out_specs=(pl.BlockSpec(memory_space=anywhere), pl.BlockSpec(memory_space=vmem)),
        scratch_shapes=[
            vmem((rows, width), jnp.bfloat16),
            vmem((rows, width), jnp.float32),
            vmem((WIN, toks, width), jnp.bfloat16),
            vmem((WIN, toks, width), jnp.bfloat16),
            vmem((2, half, width), jnp.bfloat16),
            vmem((WIN, 2, rows, half), jnp.float32),
            vmem((WIN, 2, rows, half), jnp.bfloat16),
            vmem((rows, width), jnp.float32),
            vmem((rows, width), jnp.float32),
            vmem((rows, width), jnp.float32),
            vmem((rows, width), jnp.float32),
            vmem((rows, width), jnp.float32),
            pltpu.SemaphoreType.DMA((2,)),
            pltpu.SemaphoreType.DMA,
            pltpu.SemaphoreType.DMA((2, 2)),
            pltpu.SemaphoreType.DMA((2,)),
            pltpu.SemaphoreType.DMA((2,)),
            pltpu.SemaphoreType.DMA((WIN, 4)),
            pltpu.SemaphoreType.DMA((2, 4)),
        ],
        compiler_params=pltpu.CompilerParams(collective_id=0, has_side_effects=True),
    )(
        queries.reshape(rows, width),
        keys_values.reshape(2 * toks, width),
        carry_out.reshape(rows, width),
        carry_lse,
    )
    return out.reshape(carry_out.shape), lse


def solution(mesh):
    return jax.shard_map(
        functools.partial(body, mesh.shape["ctx"]),
        mesh=mesh,
        in_specs=(
            P("ctx", "kvh", None),
            P(None, "ctx", "kvh", None),
            P("ctx", "kvh", None),
            P("kvh", "ctx"),
        ),
        out_specs=(P("ctx", "kvh", None), P("kvh", "ctx")),
        check_vma=False,
    )
```

```python
import functools
import math

import jax
import jax.numpy as jnp
from jax import lax
from jax.experimental import pallas as pl
from jax.experimental.pallas import tpu as pltpu
from jax.sharding import PartitionSpec as P

MESH = pl.DeviceIdType.MESH
WIN = 3
PLANES = 16
PIECES = 4
HANDOFF = 1
STEPS = 2
PARTS = 4


def kernel(
    n_ctx, per_group, q_hbm, kv_hbm, carry_hbm, clse_ref, out_hbm, olse_ref,
    raw, wide, q, carry_t, acc, top, total, out, inbox, blocks,
    in_sem, out_sem, own_send, hub_send, hub_recv, spread_send, recv, ready, token,
):
    toks = blocks.shape[2]
    rows_of = toks // PIECES
    lag = n_ctx // 2
    plane = n_ctx // PLANES
    deep = PLANES // 4
    me = lax.axis_index("ctx")
    kvh = lax.axis_index("kvh")
    core = lax.rem(me, 2)
    z = me // plane
    lane = lax.rem(me, plane)
    last = n_ctx - 1
    first_land = lag + 2
    high, low = deep + 1, deep - 1

    is_source = me < lag - 1
    lands = me >= first_land
    active = me >= lag + 1
    is_hub = jnp.logical_or(z == high, z == low)
    chain = z // deep
    entry = lax.rem(z, deep)
    onward = jnp.where(chain == 0, -plane, plane)
    first_plane = entry == jnp.where(chain == 0, deep - 1, 0)
    last_plane = entry == jnp.where(chain == 0, 0, deep - 1)
    follower = jnp.where(core == 0, me + 1, me + onward - 1)
    leader = jnp.where(core == 0, me - onward + 1, me - 1)
    has_follower = jnp.logical_and(
        is_source, jnp.where(core == 0, me + 1 < lag - 1, jnp.logical_not(last_plane))
    )
    has_leader = jnp.where(core == 0, jnp.logical_not(first_plane), core == 1)

    def at(device):
        return (device, kvh)

    barrier = pltpu.get_barrier_semaphore()

    def tell(device, sem=barrier):
        pl.semaphore_signal(sem, inc=1, device_id=at(device), device_id_type=MESH)

    def hub_entry(k):
        b = jnp.where(z == high, deep - 1 - k, k)
        block = (jnp.where(z == high, 0, deep) + b) * plane + lane
        return b, block, jnp.logical_and(is_hub, block < lag - 1)

    for k in range(deep):
        _, block, there = hub_entry(k)

        @pl.when(there)
        def _():
            tell(block)
            tell(jnp.minimum(block + first_land, last))

    @pl.when(jnp.logical_and(is_source, has_leader))
    def _():
        tell(leader)

    @pl.when(me > first_land)
    def _():
        tell(me - 1)

    @pl.when(jnp.logical_and(active, me < last))
    def _():
        tell(me + 1)

    peers = jnp.where(
        is_source, 1 + jnp.where(has_follower, 1, 0), jnp.where(lands, 3, 0)
    )

    @pl.when(jnp.logical_or(is_source, lands))
    def _():
        pl.semaphore_wait(barrier, peers)

    def part(p):
        return pl.ds(pl.multiple_of(p * rows_of, rows_of), rows_of)

    def own_copy(p):
        return pltpu.make_async_remote_copy(
            src_ref=kv_hbm.at[:, part(p)],
            dst_ref=inbox.at[entry, :, part(p)],
            send_sem=own_send.at[p],
            recv_sem=hub_recv.at[entry, p],
            device_id=at(jnp.where(chain == 0, high, low) * plane + lane),
            device_id_type=MESH,
        )

    def final_copy(b, block, p):
        slot = jnp.where(block == lag - 2, 2, 1)
        return pltpu.make_async_remote_copy(
            src_ref=inbox.at[b, :, part(p)],
            dst_ref=blocks.at[slot, :, part(p)],
            send_sem=hub_send.at[b, p],
            recv_sem=recv.at[slot, p],
            device_id=at(jnp.minimum(block + first_land, last)),
            device_id_type=MESH,
        )

    def send_own():
        @pl.when(has_leader)
        def _():
            pl.semaphore_wait(token, 1)

        for p in range(PIECES):
            own_copy(p).start()

        @pl.when(has_follower)
        def _():
            own_copy(HANDOFF).wait_send()
            tell(follower, token)

    def forward(i, c):
        k, p = i // PIECES, lax.rem(i, PIECES)
        b, block, there = hub_entry(k)

        @pl.when(there)
        def _():
            wait_for(inbox.at[b], hub_recv.at[b, p], p)

            @pl.when(p == 0)
            def _():
                pl.semaphore_wait(ready.at[b], 1)

            final_copy(b, block, p).start()

        return c

    def drain(i, c):
        k, p = i // PIECES, lax.rem(i, PIECES)
        b, block, there = hub_entry(k)

        @pl.when(there)
        def _():
            final_copy(b, block, p).wait_send()

        return c

    def spread_copy(to, p):
        slot, device = ((2, me - 1), (0, me + 1))[to]
        return pltpu.make_async_remote_copy(
            src_ref=blocks.at[1, :, part(p)],
            dst_ref=blocks.at[slot, :, part(p)],
            send_sem=spread_send.at[to, p],
            recv_sem=recv.at[slot, p],
            device_id=at(device),
            device_id_type=MESH,
        )

    def wait_for(buf, sem, p):
        pltpu.make_async_remote_copy(
            src_ref=buf.at[:, part(p)],
            dst_ref=buf.at[:, part(p)],
            send_sem=sem,
            recv_sem=sem,
            device_id=at(me),
            device_id_type=MESH,
        ).wait_recv()

    def allow(block):
        block_z = block // plane
        tell(
            jnp.where(block_z < deep, high, low) * plane + lax.rem(block, plane),
            ready.at[lax.rem(block_z, deep)],
        )

    @pl.when(lands)
    def _():
        allow(me - first_land)

    @pl.when(me == last)
    def _():
        allow(lag - 2)

    carry_in = pltpu.make_async_copy(carry_hbm, out, in_sem.at[0])
    q_in = pltpu.make_async_copy(q_hbm, raw, in_sem.at[1])

    def put(i):
        rows = pl.ds(i * (out.shape[0] // PARTS), out.shape[0] // PARTS)
        return pltpu.make_async_copy(out.at[rows], out_hbm.at[rows], out_sem.at[i])

    carry_in.start()

    @pl.when(active)
    def _():
        q_in.start()

    @pl.when(jnp.logical_not(active))
    def _():
        olse_ref[...] = clse_ref[...]
        carry_in.wait()
        for i in range(PARTS):
            put(i).start()

    @pl.when(is_source)
    def _():
        send_own()

    @pl.when(is_hub)
    def _():
        lax.fori_loop(0, deep * PIECES, forward, 0)

    @pl.when(active)
    def _():
        top[...] = jnp.full(top.shape, -jnp.inf, jnp.float32)
        total[...] = jnp.zeros(total.shape, jnp.float32)
        acc[...] = jnp.zeros(acc.shape, jnp.float32)
        q_in.wait()
        wide[...] = raw[...].astype(jnp.float32)
        for h in range(per_group):
            q[h] = wide[pl.ds(h, toks, stride=per_group), :].astype(jnp.bfloat16)
        carry_in.wait()
        for h in range(per_group):
            carry_t[h] = jnp.transpose(out[pl.ds(h, toks, stride=per_group), :])

    scale = q.shape[2] ** -0.5
    in_two = scale * math.log2(math.e)

    def attend(slot, p):
        rows = pl.ds(p * (toks // STEPS), toks // STEPS)
        keys = blocks[slot, 0, rows, :]
        values_t = jnp.transpose(blocks[slot, 1, rows, :])

        def head(h, c):
            s = lax.dot_general(
                keys, q[h], (((1,), (1,)), ((), ())), preferred_element_type=jnp.float32
            )
            old = top[h]
            new = jnp.maximum(old, jnp.max(s, axis=0, keepdims=True))
            weights = jnp.exp2((s - new) * in_two)
            shrink = jnp.exp2((old - new) * in_two)
            total[h] = total[h] * shrink + jnp.sum(weights, axis=0, keepdims=True)
            acc[h] = acc[h] * shrink + jnp.dot(
                values_t, weights.astype(jnp.bfloat16), preferred_element_type=jnp.float32
            )
            top[h] = new
            return c

        lax.fori_loop(0, per_group, head, 0, unroll=True)

    mate = jnp.where(core == 0, 2, 0)
    other = jnp.where(core == 0, 0, 2)

    def land(step):
        @pl.when(lands)
        def _():
            for p in pieces_of(step):
                wait_for(blocks.at[1], recv.at[1, p], p)
                spread_copy(0, p).start()

                @pl.when(me < last)
                def _():
                    spread_copy(1, p).start()

    def attend_mid(step):
        @pl.when(lands)
        def _():
            attend(1, step)

    def attend_from(slot, step):
        @pl.when(jnp.logical_and(active, me - lag - WIN + slot >= 0))
        def _():
            for p in pieces_of(step):
                wait_for(blocks.at[slot], recv.at[slot, p], p)
            attend(slot, step)

    def pieces_of(step):
        per_step = PIECES // STEPS
        return range(step * per_step, (step + 1) * per_step)

    land(0)
    attend_mid(0)
    attend_from(mate, 0)
    land(1)
    attend_from(other, 0)
    attend_mid(1)
    attend_from(mate, 1)
    attend_from(other, 1)

    @pl.when(active)
    def _():
        for h in range(per_group):
            weight_sum = total[h]
            window_lse = top[h] * scale + jnp.log(weight_sum)
            before = clse_ref[pl.ds(h, 1), :]
            ceiling = jnp.maximum(before, window_lse)
            merged = ceiling + jnp.log(
                jnp.exp(before - ceiling) + jnp.exp(window_lse - ceiling)
            )
            olse_ref[pl.ds(h, 1), :] = merged
            top[h] = jnp.exp(window_lse - merged) / weight_sum
            total[h] = jnp.exp(before - merged)
        some = toks // PARTS
        for i in range(PARTS):
            cols = pl.ds(i * some, some)
            for h in range(per_group):
                result = acc[h, :, cols] * top[h, :, cols] + carry_t[h, :, cols] * total[h, :, cols]
                out[pl.ds(i * some * per_group + h, some, stride=per_group), :] = (
                    jnp.transpose(result)
                )
            put(i).start()

    @pl.when(is_source)
    def _():
        for p in range(PIECES):
            if p != HANDOFF:
                own_copy(p).wait_send()

        @pl.when(jnp.logical_not(has_follower))
        def _():
            own_copy(HANDOFF).wait_send()

    @pl.when(is_hub)
    def _():
        lax.fori_loop(0, deep * PIECES, drain, 0)

    @pl.when(lands)
    def _():
        for p in range(PIECES):
            spread_copy(0, p).wait_send()

            @pl.when(me < last)
            def _():
                spread_copy(1, p).wait_send()

    for i in range(PARTS):
        put(i).wait()


def body(n_ctx, queries, keys_values, carry_out, carry_lse):
    toks, heads, width = queries.shape
    group = heads // keys_values.shape[2]
    rows = toks * heads
    deep = PLANES // 4
    vmem, anywhere, dma = pltpu.VMEM, pl.ANY, pltpu.SemaphoreType.DMA
    out, lse = pl.pallas_call(
        functools.partial(kernel, n_ctx, group),
        name="window_attention",
        out_shape=(
            jax.ShapeDtypeStruct((rows, width), jnp.float32),
            jax.ShapeDtypeStruct(carry_lse.shape, jnp.float32),
        ),
        in_specs=[
            pl.BlockSpec(memory_space=anywhere),
            pl.BlockSpec(memory_space=anywhere),
            pl.BlockSpec(memory_space=anywhere),
            pl.BlockSpec(memory_space=vmem),
        ],
        out_specs=(pl.BlockSpec(memory_space=anywhere), pl.BlockSpec(memory_space=vmem)),
        scratch_shapes=[
            vmem((rows, width), jnp.bfloat16),
            vmem((rows, width), jnp.float32),
            vmem((group, toks, width), jnp.bfloat16),
            vmem((group, width, toks), jnp.float32),
            vmem((group, width, toks), jnp.float32),
            vmem((group, 1, toks), jnp.float32),
            vmem((group, 1, toks), jnp.float32),
            vmem((rows, width), jnp.float32),
            vmem((deep, 2, toks, width), jnp.bfloat16),
            vmem((WIN, 2, toks, width), jnp.bfloat16),
            dma((2,)),
            dma((PARTS,)),
            dma((PIECES,)),
            dma((deep, PIECES)),
            dma((deep, PIECES)),
            dma((2, PIECES)),
            dma((WIN, PIECES)),
            pltpu.SemaphoreType.REGULAR((deep,)),
            pltpu.SemaphoreType.REGULAR,
        ],
        compiler_params=pltpu.CompilerParams(collective_id=0, has_side_effects=True),
    )(
        queries.reshape(rows, width),
        keys_values.reshape(2, toks, width),
        carry_out.reshape(rows, width),
        carry_lse,
    )
    return out.reshape(carry_out.shape), lse


def solution(mesh):
    return jax.shard_map(
        functools.partial(body, mesh.shape["ctx"]),
        mesh=mesh,
        in_specs=(
            P("ctx", "kvh", None),
            P(None, "ctx", "kvh", None),
            P("ctx", "kvh", None),
            P("kvh", "ctx"),
        ),
        out_specs=(P("ctx", "kvh", None), P("kvh", "ctx")),
        check_vma=False,
    )
```

```python
import functools
import math

import jax
import jax.numpy as jnp
from jax import lax
from jax.experimental import pallas as pl
from jax.experimental.pallas import tpu as pltpu
from jax.sharding import PartitionSpec as P

MESH = pl.DeviceIdType.MESH
WIN = 3
PLANES = 16
PIECES = 4
HANDOFF = 0
STEPS = 2
PARTS = 4


def kernel(
    n_ctx, per_group, q_hbm, kv_hbm, carry_hbm, clse_hbm, out, olse_ref,
    raw, wide, q, carry_t, acc, top, total, clse_ref, inbox, blocks,
    in_sem, own_send, hub_send, hub_recv, spread_send, recv, ready, token,
):
    toks = blocks.shape[2]
    rows_of = toks // PIECES
    lag = n_ctx // 2
    plane = n_ctx // PLANES
    deep = PLANES // 4
    me = lax.axis_index("ctx")
    kvh = lax.axis_index("kvh")
    core = lax.rem(me, 2)
    z = me // plane
    lane = lax.rem(me, plane)
    last = n_ctx - 1
    split = plane - 2
    high, low = deep + 1, deep - 1

    is_source = me < lag - 1
    has_mid = me >= lag + 2
    lands_mid = jnp.logical_and(has_mid, lane != 0)
    lands_high = jnp.logical_and(me >= lag + 1, lane == plane - 1)
    active = me >= lag + 1
    is_hub = jnp.logical_or(z == high, z == low)
    direct = jnp.logical_and(z == low, lane > split)
    stages = jnp.logical_and(is_source, jnp.logical_not(direct))
    chain = z // deep
    entry = lax.rem(z, deep)
    onward = jnp.where(chain == 0, -plane, plane)
    first_plane = entry == jnp.where(chain == 0, jnp.where(lane <= split, deep - 1, deep - 2), 0)
    last_plane = entry == jnp.where(chain == 0, 0, deep - 1)
    follower = jnp.where(core == 0, me + 1, me + onward - 1)
    leader = jnp.where(core == 0, me - onward + 1, me - 1)
    follower = jnp.where(jnp.logical_and(z == low, lane == split), me + onward, follower)
    leader = jnp.where(jnp.logical_and(z == low - 1, lane == split), me - onward, leader)
    has_follower = jnp.logical_and(
        stages, jnp.where(core == 0, me + 1 < lag - 1, jnp.logical_not(last_plane))
    )
    has_leader = jnp.logical_and(
        stages, jnp.logical_or(core == 1, jnp.logical_not(first_plane))
    )

    def at(device):
        return (device, kvh)

    barrier = pltpu.get_barrier_semaphore()

    def tell(device, sem=barrier):
        pl.semaphore_signal(sem, inc=1, device_id=at(device), device_id_type=MESH)

    def hub_entry(k):
        b = jnp.where(z == high, deep - 1 - k, k)
        block = (jnp.where(z == high, 0, deep) + b) * plane + lane
        there = jnp.logical_and(is_hub, block < lag - 1)
        elsewhere = jnp.logical_and(block // plane == low, lane > split)
        return b, block, jnp.logical_and(there, jnp.logical_not(elsewhere))

    landing = jnp.where(lane == split, 1, 2)

    for k in range(deep):
        _, block, there = hub_entry(k)

        @pl.when(there)
        def _():
            tell(block)
            tell(jnp.minimum(block + lag + landing, last))

    @pl.when(has_leader)
    def _():
        tell(leader)

    @pl.when(direct)
    def _():
        tell(me + lag + landing)

    @pl.when(me >= lag + WIN)
    def _():
        tell(me - 1)

    @pl.when(jnp.logical_and(active, lane != plane - 1))
    def _():
        tell(me + 1)

    def one_if(condition):
        return jnp.where(condition, 1, 0)

    peers = (
        one_if(stages)
        + one_if(has_follower)
        + one_if(lands_mid) * 2
        + one_if(jnp.logical_and(has_mid, me < last))
        + one_if(lands_high)
    )

    @pl.when(peers > 0)
    def _():
        pl.semaphore_wait(barrier, peers)

    def part(p):
        return pl.ds(pl.multiple_of(p * rows_of, rows_of), rows_of)

    def own_copy(p):
        return pltpu.make_async_remote_copy(
            src_ref=kv_hbm.at[:, part(p)],
            dst_ref=inbox.at[entry, :, part(p)],
            send_sem=own_send.at[p],
            recv_sem=hub_recv.at[entry, p],
            device_id=at(jnp.where(chain == 0, high, low) * plane + lane),
            device_id_type=MESH,
        )

    def direct_copy(p):
        slot = jnp.where(lane == split, 2, 1)
        return pltpu.make_async_remote_copy(
            src_ref=kv_hbm.at[:, part(p)],
            dst_ref=blocks.at[slot, :, part(p)],
            send_sem=own_send.at[p],
            recv_sem=recv.at[slot, p],
            device_id=at(jnp.minimum(me + lag + landing, last)),
            device_id_type=MESH,
        )

    def final_copy(b, block, p):
        slot = jnp.where(lane == split, 2, 1)
        return pltpu.make_async_remote_copy(
            src_ref=inbox.at[b, :, part(p)],
            dst_ref=blocks.at[slot, :, part(p)],
            send_sem=hub_send.at[b, p],
            recv_sem=recv.at[slot, p],
            device_id=at(jnp.minimum(block + lag + landing, last)),
            device_id_type=MESH,
        )

    def send_own():
        @pl.when(has_leader)
        def _():
            pl.semaphore_wait(token, 1)

        for p in range(PIECES):
            own_copy(p).start()

        @pl.when(has_follower)
        def _():
            own_copy(HANDOFF).wait_send()
            tell(follower, token)

    def forward(i, c):
        k, p = i // PIECES, lax.rem(i, PIECES)
        b, block, there = hub_entry(k)

        @pl.when(there)
        def _():
            wait_for(inbox.at[b], hub_recv.at[b, p], p)

            @pl.when(p == 0)
            def _():
                pl.semaphore_wait(ready.at[b], 1)

            final_copy(b, block, p).start()

        return c

    def drain(i, c):
        k, p = i // PIECES, lax.rem(i, PIECES)
        b, block, there = hub_entry(k)

        @pl.when(there)
        def _():
            final_copy(b, block, p).wait_send()

        return c

    spreads = ((1, 2, me - 1), (1, 0, me + 1), (2, 1, me + 1))
    spread_there = (
        lands_mid,
        jnp.logical_and(has_mid, me < last),
        jnp.logical_and(lands_high, me < last),
    )

    def spread_copy(to, p):
        landed, slot, device = spreads[to]
        return pltpu.make_async_remote_copy(
            src_ref=blocks.at[landed, :, part(p)],
            dst_ref=blocks.at[slot, :, part(p)],
            send_sem=spread_send.at[to, p],
            recv_sem=recv.at[slot, p],
            device_id=at(device),
            device_id_type=MESH,
        )

    def wait_for(buf, sem, p):
        pltpu.make_async_remote_copy(
            src_ref=buf.at[:, part(p)],
            dst_ref=buf.at[:, part(p)],
            send_sem=sem,
            recv_sem=sem,
            device_id=at(me),
            device_id_type=MESH,
        ).wait_recv()

    def allow(block):
        block_z, block_lane = block // plane, lax.rem(block, plane)
        by_owner = jnp.logical_and(block_z == low, block_lane > split)

        @pl.when(by_owner)
        def _():
            tell(block, ready.at[deep])

        @pl.when(jnp.logical_not(by_owner))
        def _():
            hub_z = jnp.where(block_z < deep, high, low)
            tell(hub_z * plane + block_lane, ready.at[lax.rem(block_z, deep)])

    @pl.when(lands_mid)
    def _():
        allow(me - lag - 2)

    @pl.when(lands_high)
    def _():
        allow(me - lag - 1)

    carry_in = pltpu.make_async_copy(carry_hbm, out, in_sem.at[0])
    q_in = pltpu.make_async_copy(q_hbm, raw, in_sem.at[1])

    clse_in = pltpu.make_async_copy(clse_hbm, clse_ref, in_sem.at[2])
    carry_in.start()
    clse_in.start()

    @pl.when(active)
    def _():
        q_in.start()

    @pl.when(jnp.logical_not(active))
    def _():
        clse_in.wait()
        olse_ref[...] = clse_ref[...]
        carry_in.wait()

    @pl.when(stages)
    def _():
        send_own()

    @pl.when(direct)
    def _():
        pl.semaphore_wait(ready.at[deep], 1)
        for p in range(PIECES):
            direct_copy(p).start()

    @pl.when(is_hub)
    def _():
        lax.fori_loop(0, deep * PIECES, forward, 0)

    @pl.when(active)
    def _():
        top[...] = jnp.full(top.shape, -jnp.inf, jnp.float32)
        total[...] = jnp.zeros(total.shape, jnp.float32)
        acc[...] = jnp.zeros(acc.shape, jnp.float32)
        q_in.wait()
        clse_in.wait()
        wide[...] = raw[...].astype(jnp.float32)
        for h in range(per_group):
            q[h] = wide[pl.ds(h, toks, stride=per_group), :].astype(jnp.bfloat16)
        carry_in.wait()
        for h in range(per_group):
            carry_t[h] = jnp.transpose(out[pl.ds(h, toks, stride=per_group), :])

    scale = q.shape[2] ** -0.5
    in_two = scale * math.log2(math.e)

    def attend(slot, p):
        rows = pl.ds(p * (toks // STEPS), toks // STEPS)
        keys = blocks[slot, 0, rows, :]
        values_t = jnp.transpose(blocks[slot, 1, rows, :])

        def head(h, c):
            s = lax.dot_general(
                keys, q[h], (((1,), (1,)), ((), ())), preferred_element_type=jnp.float32
            )
            old = top[h]
            new = jnp.maximum(old, jnp.max(s, axis=0, keepdims=True))
            weights = jnp.exp2((s - new) * in_two)
            shrink = jnp.exp2((old - new) * in_two)
            total[h] = total[h] * shrink + jnp.sum(weights, axis=0, keepdims=True)
            acc[h] = acc[h] * shrink + jnp.dot(
                values_t, weights.astype(jnp.bfloat16), preferred_element_type=jnp.float32
            )
            top[h] = new
            return c

        lax.fori_loop(0, per_group, head, 0, unroll=True)

    def take(slot, copies, there, pieces):
        @pl.when(there)
        def _():
            for p in pieces:
                wait_for(blocks.at[slot], recv.at[slot, p], p)
                for to in copies:

                    @pl.when(spread_there[to])
                    def _():
                        spread_copy(to, p).start()

    def land(step):
        take(1, (0, 1), lands_mid, pieces_of(step))

    def attend_from(slot, step):
        @pl.when(jnp.logical_and(active, me - lag - WIN + slot >= 0))
        def _():
            landed = jnp.logical_or(slot == 1, jnp.logical_and(slot == 2, lands_high))

            @pl.when(jnp.logical_not(landed))
            def _():
                for p in pieces_of(step):
                    wait_for(blocks.at[slot], recv.at[slot, p], p)

            attend(slot, step)

    def pieces_of(step):
        per_step = PIECES // STEPS
        return range(step * per_step, (step + 1) * per_step)

    starts_plane = lane == 0
    second = jnp.where(core == 1, 0, 2)
    third = jnp.where(core == 0, 0, 2)

    def ahead(step):
        @pl.when(starts_plane)
        def _():
            attend_from(2, step)

    def second_from(step):
        @pl.when(jnp.logical_not(starts_plane))
        def _():
            attend_from(second, step)

    take(2, (2,), lands_high, range(PIECES))
    take(1, (1,), jnp.logical_and(has_mid, starts_plane), range(PIECES))
    ahead(0)
    land(0)
    attend_from(1, 0)
    second_from(0)
    ahead(1)
    land(1)
    attend_from(third, 0)
    attend_from(1, 1)
    second_from(1)
    attend_from(third, 1)

    @pl.when(active)
    def _():
        for h in range(per_group):
            weight_sum = total[h]
            window_lse = top[h] * scale + jnp.log(weight_sum)
            before = clse_ref[pl.ds(h, 1), :]
            ceiling = jnp.maximum(before, window_lse)
            merged = ceiling + jnp.log(
                jnp.exp(before - ceiling) + jnp.exp(window_lse - ceiling)
            )
            olse_ref[pl.ds(h, 1), :] = merged
            top[h] = jnp.exp(window_lse - merged) / weight_sum
            total[h] = jnp.exp(before - merged)
        some = toks // PARTS
        for i in range(PARTS):
            cols = pl.ds(i * some, some)
            for h in range(per_group):
                result = acc[h, :, cols] * top[h, :, cols] + carry_t[h, :, cols] * total[h, :, cols]
                out[pl.ds(i * some * per_group + h, some, stride=per_group), :] = (
                    jnp.transpose(result)
                )

    @pl.when(direct)
    def _():
        for p in range(PIECES):
            direct_copy(p).wait_send()

    @pl.when(stages)
    def _():
        for p in range(PIECES):
            if p != HANDOFF:
                own_copy(p).wait_send()

        @pl.when(jnp.logical_not(has_follower))
        def _():
            own_copy(HANDOFF).wait_send()

    @pl.when(is_hub)
    def _():
        lax.fori_loop(0, deep * PIECES, drain, 0)

    for to in range(3):

        @pl.when(spread_there[to])
        def _():
            for p in range(PIECES):
                spread_copy(to, p).wait_send()


def in_hbm(array):
    return pltpu.with_memory_space_constraint(array, pltpu.HBM)


def body(n_ctx, queries, keys_values, carry_out, carry_lse):
    toks, heads, width = queries.shape
    group = heads // keys_values.shape[2]
    rows = toks * heads
    deep = PLANES // 4
    vmem, dma = pltpu.VMEM, pltpu.SemaphoreType.DMA
    out, lse = pl.pallas_call(
        functools.partial(kernel, n_ctx, group),
        name="window_attention",
        out_shape=(
            jax.ShapeDtypeStruct((rows, width), jnp.float32),
            jax.ShapeDtypeStruct(carry_lse.shape, jnp.float32),
        ),
        in_specs=[
            pl.BlockSpec(memory_space=pltpu.HBM),
            pl.BlockSpec(memory_space=pltpu.HBM),
            pl.BlockSpec(memory_space=pltpu.HBM),
            pl.BlockSpec(memory_space=pltpu.HBM),
        ],
        out_specs=(pl.BlockSpec(memory_space=vmem), pl.BlockSpec(memory_space=vmem)),
        scratch_shapes=[
            vmem((rows, width), jnp.bfloat16),
            vmem((rows, width), jnp.float32),
            vmem((group, toks, width), jnp.bfloat16),
            vmem((group, width, toks), jnp.float32),
            vmem((group, width, toks), jnp.float32),
            vmem((group, 1, toks), jnp.float32),
            vmem((group, 1, toks), jnp.float32),
            vmem(carry_lse.shape, jnp.float32),
            vmem((deep, 2, toks, width), jnp.bfloat16),
            vmem((WIN, 2, toks, width), jnp.bfloat16),
            dma((3,)),
            dma((PIECES,)),
            dma((deep, PIECES)),
            dma((deep, PIECES)),
            dma((3, PIECES)),
            dma((WIN, PIECES)),
            pltpu.SemaphoreType.REGULAR((deep + 1,)),
            pltpu.SemaphoreType.REGULAR,
        ],
        compiler_params=pltpu.CompilerParams(
            collective_id=0, has_side_effects=True, vmem_limit_bytes=24 * 2**20
        ),
    )(
        in_hbm(queries.reshape(rows, width)),
        in_hbm(keys_values.reshape(2, toks, width)),
        in_hbm(carry_out.reshape(rows, width)),
        in_hbm(carry_lse),
    )
    return out.reshape(carry_out.shape), lse


def solution(mesh):
    return jax.shard_map(
        functools.partial(body, mesh.shape["ctx"]),
        mesh=mesh,
        in_specs=(
            P("ctx", "kvh", None),
            P(None, "ctx", "kvh", None),
            P("ctx", "kvh", None),
            P("kvh", "ctx"),
        ),
        out_specs=(P("ctx", "kvh", None), P("kvh", "ctx")),
        check_vma=False,
    )
```

```python
import functools
import math

import jax
import jax.numpy as jnp
from jax import lax
from jax.experimental import pallas as pl
from jax.experimental.pallas import tpu as pltpu
from jax.sharding import PartitionSpec as P

MESH = pl.DeviceIdType.MESH
WIN = 3
PLANES = 16
PIECES = 4
HANDOFF = 0
STEPS = 2
PARTS = 4


def kernel(
    n_ctx, per_group, q_hbm, kv_hbm, carry_hbm, clse_hbm, out, olse_ref,
    raw, wide, q, carry_t, acc, top, total, clse_ref, inbox, blocks,
    in_sem, own_send, hub_send, hub_recv, spread_send, recv, ready, token,
):
    toks = blocks.shape[2]
    rows_of = toks // PIECES
    lag = n_ctx // 2
    plane = n_ctx // PLANES
    deep = PLANES // 4
    me = lax.axis_index("ctx")
    kvh = lax.axis_index("kvh")
    core = lax.rem(me, 2)
    z = me // plane
    lane = lax.rem(me, plane)
    last = n_ctx - 1
    split = plane - 2
    high, low = deep + 1, deep - 1

    is_source = me < lag - 1
    has_mid = me >= lag + 2
    lands_mid = jnp.logical_and(has_mid, lane != 0)
    lands_high = jnp.logical_and(me >= lag + 1, lane == plane - 1)
    active = me >= lag + 1
    is_hub = jnp.logical_or(z == high, z == low)
    direct = jnp.logical_and(z == 0, lane >= split)
    stages = jnp.logical_and(is_source, jnp.logical_not(direct))
    chain = z // deep
    entry = lax.rem(z, deep)
    onward = jnp.where(chain == 0, -plane, plane)
    first_plane = entry == jnp.where(chain == 0, deep - 1, 0)
    last_plane = entry == jnp.where(chain == 0, jnp.where(lane < split, 0, 1), deep - 1)
    follower = jnp.where(core == 0, me + 1, me + onward - 1)
    leader = jnp.where(core == 0, me - onward + 1, me - 1)
    has_follower = jnp.logical_and(
        stages, jnp.where(core == 0, me + 1 < lag - 1, jnp.logical_not(last_plane))
    )
    has_leader = jnp.logical_and(
        stages, jnp.logical_or(core == 1, jnp.logical_not(first_plane))
    )

    def at(device):
        return (device, kvh)

    barrier = pltpu.get_barrier_semaphore()

    def tell(device, sem=barrier):
        pl.semaphore_signal(sem, inc=1, device_id=at(device), device_id_type=MESH)

    def hub_entry(k):
        b = jnp.where(z == high, deep - 1 - k, k)
        block = (jnp.where(z == high, 0, deep) + b) * plane + lane
        there = jnp.logical_and(is_hub, block < lag - 1)
        elsewhere = jnp.logical_and(block // plane == 0, lane >= split)
        return b, block, jnp.logical_and(there, jnp.logical_not(elsewhere))

    landing = jnp.where(lane == split, 1, 2)

    for k in range(deep):
        _, block, there = hub_entry(k)

        @pl.when(there)
        def _():
            tell(block)
            tell(jnp.minimum(block + lag + landing, last))

    @pl.when(has_leader)
    def _():
        tell(leader)

    @pl.when(direct)
    def _():
        tell(me + lag + landing)

    @pl.when(me >= lag + WIN)
    def _():
        tell(me - 1)

    @pl.when(jnp.logical_and(active, lane != plane - 1))
    def _():
        tell(me + 1)

    def one_if(condition):
        return jnp.where(condition, 1, 0)

    peers = (
        one_if(stages)
        + one_if(has_follower)
        + one_if(lands_mid) * 2
        + one_if(jnp.logical_and(has_mid, me < last))
        + one_if(lands_high)
    )

    @pl.when(peers > 0)
    def _():
        pl.semaphore_wait(barrier, peers)

    def part(p):
        return pl.ds(pl.multiple_of(p * rows_of, rows_of), rows_of)

    def own_copy(p):
        return pltpu.make_async_remote_copy(
            src_ref=kv_hbm.at[:, part(p)],
            dst_ref=inbox.at[entry, :, part(p)],
            send_sem=own_send.at[p],
            recv_sem=hub_recv.at[entry, p],
            device_id=at(jnp.where(chain == 0, high, low) * plane + lane),
            device_id_type=MESH,
        )

    def direct_copy(p):
        slot = jnp.where(lane == split, 2, 1)
        return pltpu.make_async_remote_copy(
            src_ref=kv_hbm.at[:, part(p)],
            dst_ref=blocks.at[slot, :, part(p)],
            send_sem=own_send.at[p],
            recv_sem=recv.at[slot, p],
            device_id=at(jnp.minimum(me + lag + landing, last)),
            device_id_type=MESH,
        )

    def final_copy(b, block, p):
        slot = jnp.where(lane == split, 2, 1)
        return pltpu.make_async_remote_copy(
            src_ref=inbox.at[b, :, part(p)],
            dst_ref=blocks.at[slot, :, part(p)],
            send_sem=hub_send.at[b, p],
            recv_sem=recv.at[slot, p],
            device_id=at(jnp.minimum(block + lag + landing, last)),
            device_id_type=MESH,
        )

    def send_own():
        @pl.when(has_leader)
        def _():
            pl.semaphore_wait(token, 1)

        for p in range(PIECES):
            own_copy(p).start()

        @pl.when(has_follower)
        def _():
            own_copy(HANDOFF).wait_send()
            tell(follower, token)

    def forward(i, c):
        k, p = i // PIECES, lax.rem(i, PIECES)
        b, block, there = hub_entry(k)

        @pl.when(there)
        def _():
            wait_for(inbox.at[b], hub_recv.at[b, p], p)

            @pl.when(p == 0)
            def _():
                pl.semaphore_wait(ready.at[b], 1)

            final_copy(b, block, p).start()

        return c

    def drain(i, c):
        k, p = i // PIECES, lax.rem(i, PIECES)
        b, block, there = hub_entry(k)

        @pl.when(there)
        def _():
            final_copy(b, block, p).wait_send()

        return c

    spreads = ((1, 2, me - 1), (1, 0, me + 1), (2, 1, me + 1))
    spread_there = (
        lands_mid,
        jnp.logical_and(has_mid, me < last),
        jnp.logical_and(lands_high, me < last),
    )

    def spread_copy(to, p):
        landed, slot, device = spreads[to]
        return pltpu.make_async_remote_copy(
            src_ref=blocks.at[landed, :, part(p)],
            dst_ref=blocks.at[slot, :, part(p)],
            send_sem=spread_send.at[to, p],
            recv_sem=recv.at[slot, p],
            device_id=at(device),
            device_id_type=MESH,
        )

    def wait_for(buf, sem, p):
        pltpu.make_async_remote_copy(
            src_ref=buf.at[:, part(p)],
            dst_ref=buf.at[:, part(p)],
            send_sem=sem,
            recv_sem=sem,
            device_id=at(me),
            device_id_type=MESH,
        ).wait_recv()

    def allow(block):
        block_z, block_lane = block // plane, lax.rem(block, plane)
        by_owner = jnp.logical_and(block_z == 0, block_lane >= split)

        @pl.when(by_owner)
        def _():
            tell(block, ready.at[deep])

        @pl.when(jnp.logical_not(by_owner))
        def _():
            hub_z = jnp.where(block_z < deep, high, low)
            tell(hub_z * plane + block_lane, ready.at[lax.rem(block_z, deep)])

    @pl.when(lands_mid)
    def _():
        allow(me - lag - 2)

    @pl.when(lands_high)
    def _():
        allow(me - lag - 1)

    carry_in = pltpu.make_async_copy(carry_hbm, out, in_sem.at[0])
    q_in = pltpu.make_async_copy(q_hbm, raw, in_sem.at[1])

    clse_in = pltpu.make_async_copy(clse_hbm, clse_ref, in_sem.at[2])
    carry_in.start()
    clse_in.start()

    @pl.when(active)
    def _():
        q_in.start()

    @pl.when(jnp.logical_not(active))
    def _():
        clse_in.wait()
        olse_ref[...] = clse_ref[...]
        carry_in.wait()

    @pl.when(stages)
    def _():
        send_own()

    @pl.when(direct)
    def _():
        pl.semaphore_wait(ready.at[deep], 1)
        for p in range(PIECES):
            direct_copy(p).start()

    @pl.when(is_hub)
    def _():
        lax.fori_loop(0, deep * PIECES, forward, 0)

    @pl.when(active)
    def _():
        top[...] = jnp.full(top.shape, -jnp.inf, jnp.float32)
        total[...] = jnp.zeros(total.shape, jnp.float32)
        acc[...] = jnp.zeros(acc.shape, jnp.float32)
        q_in.wait()
        clse_in.wait()
        wide[...] = raw[...].astype(jnp.float32)
        for h in range(per_group):
            q[h] = wide[pl.ds(h, toks, stride=per_group), :].astype(jnp.bfloat16)
        carry_in.wait()
        for h in range(per_group):
            carry_t[h] = jnp.transpose(out[pl.ds(h, toks, stride=per_group), :])

    scale = q.shape[2] ** -0.5
    in_two = scale * math.log2(math.e)

    def attend(slot, p):
        rows = pl.ds(p * (toks // STEPS), toks // STEPS)
        keys = blocks[slot, 0, rows, :]
        values_t = jnp.transpose(blocks[slot, 1, rows, :])

        def head(h, c):
            s = lax.dot_general(
                keys, q[h], (((1,), (1,)), ((), ())), preferred_element_type=jnp.float32
            )
            old = top[h]
            new = jnp.maximum(old, jnp.max(s, axis=0, keepdims=True))
            weights = jnp.exp2((s - new) * in_two)
            shrink = jnp.exp2((old - new) * in_two)
            total[h] = total[h] * shrink + jnp.sum(weights, axis=0, keepdims=True)
            acc[h] = acc[h] * shrink + jnp.dot(
                values_t, weights.astype(jnp.bfloat16), preferred_element_type=jnp.float32
            )
            top[h] = new
            return c

        lax.fori_loop(0, per_group, head, 0, unroll=True)

    def take(slot, copies, there, pieces):
        @pl.when(there)
        def _():
            for p in pieces:
                wait_for(blocks.at[slot], recv.at[slot, p], p)
                for to in copies:

                    @pl.when(spread_there[to])
                    def _():
                        spread_copy(to, p).start()

    def land(step):
        take(1, (0, 1), lands_mid, pieces_of(step))

    def attend_from(slot, step):
        @pl.when(jnp.logical_and(active, me - lag - WIN + slot >= 0))
        def _():
            landed = jnp.logical_or(slot == 1, jnp.logical_and(slot == 2, lands_high))

            @pl.when(jnp.logical_not(landed))
            def _():
                for p in pieces_of(step):
                    wait_for(blocks.at[slot], recv.at[slot, p], p)

            attend(slot, step)

    def pieces_of(step):
        per_step = PIECES // STEPS
        return range(step * per_step, (step + 1) * per_step)

    starts_plane = lane == 0
    second = jnp.where(core == 1, 0, 2)
    third = jnp.where(core == 0, 0, 2)

    def ahead(step):
        @pl.when(starts_plane)
        def _():
            attend_from(2, step)

    def second_from(step):
        @pl.when(jnp.logical_not(starts_plane))
        def _():
            attend_from(second, step)

    take(2, (2,), lands_high, range(PIECES))
    take(1, (1,), jnp.logical_and(has_mid, starts_plane), range(PIECES))
    ahead(0)
    land(0)
    attend_from(1, 0)
    second_from(0)
    ahead(1)
    land(1)
    attend_from(third, 0)
    attend_from(1, 1)
    second_from(1)
    attend_from(third, 1)

    @pl.when(active)
    def _():
        for h in range(per_group):
            weight_sum = total[h]
            window_lse = top[h] * scale + jnp.log(weight_sum)
            before = clse_ref[pl.ds(h, 1), :]
            ceiling = jnp.maximum(before, window_lse)
            merged = ceiling + jnp.log(
                jnp.exp(before - ceiling) + jnp.exp(window_lse - ceiling)
            )
            olse_ref[pl.ds(h, 1), :] = merged
            top[h] = jnp.exp(window_lse - merged) / weight_sum
            total[h] = jnp.exp(before - merged)
        some = toks // PARTS
        for i in range(PARTS):
            cols = pl.ds(i * some, some)
            for h in range(per_group):
                result = acc[h, :, cols] * top[h, :, cols] + carry_t[h, :, cols] * total[h, :, cols]
                out[pl.ds(i * some * per_group + h, some, stride=per_group), :] = (
                    jnp.transpose(result)
                )

    @pl.when(direct)
    def _():
        for p in range(PIECES):
            direct_copy(p).wait_send()

    @pl.when(stages)
    def _():
        for p in range(PIECES):
            if p != HANDOFF:
                own_copy(p).wait_send()

        @pl.when(jnp.logical_not(has_follower))
        def _():
            own_copy(HANDOFF).wait_send()

    @pl.when(is_hub)
    def _():
        lax.fori_loop(0, deep * PIECES, drain, 0)

    for to in range(3):

        @pl.when(spread_there[to])
        def _():
            for p in range(PIECES):
                spread_copy(to, p).wait_send()


def in_hbm(array):
    return pltpu.with_memory_space_constraint(array, pltpu.HBM)


def body(n_ctx, queries, keys_values, carry_out, carry_lse):
    toks, heads, width = queries.shape
    group = heads // keys_values.shape[2]
    rows = toks * heads
    deep = PLANES // 4
    vmem, dma = pltpu.VMEM, pltpu.SemaphoreType.DMA
    out, lse = pl.pallas_call(
        functools.partial(kernel, n_ctx, group),
        name="window_attention",
        out_shape=(
            jax.ShapeDtypeStruct((rows, width), jnp.float32),
            jax.ShapeDtypeStruct(carry_lse.shape, jnp.float32),
        ),
        in_specs=[
            pl.BlockSpec(memory_space=pltpu.HBM),
            pl.BlockSpec(memory_space=pltpu.HBM),
            pl.BlockSpec(memory_space=pltpu.HBM),
            pl.BlockSpec(memory_space=pltpu.HBM),
        ],
        out_specs=(pl.BlockSpec(memory_space=vmem), pl.BlockSpec(memory_space=vmem)),
        scratch_shapes=[
            vmem((rows, width), jnp.bfloat16),
            vmem((rows, width), jnp.float32),
            vmem((group, toks, width), jnp.bfloat16),
            vmem((group, width, toks), jnp.float32),
            vmem((group, width, toks), jnp.float32),
            vmem((group, 1, toks), jnp.float32),
            vmem((group, 1, toks), jnp.float32),
            vmem(carry_lse.shape, jnp.float32),
            vmem((deep, 2, toks, width), jnp.bfloat16),
            vmem((WIN, 2, toks, width), jnp.bfloat16),
            dma((3,)),
            dma((PIECES,)),
            dma((deep, PIECES)),
            dma((deep, PIECES)),
            dma((3, PIECES)),
            dma((WIN, PIECES)),
            pltpu.SemaphoreType.REGULAR((deep + 1,)),
            pltpu.SemaphoreType.REGULAR,
        ],
        compiler_params=pltpu.CompilerParams(
            collective_id=0, has_side_effects=True, vmem_limit_bytes=24 * 2**20
        ),
    )(
        in_hbm(queries.reshape(rows, width)),
        in_hbm(keys_values.reshape(2, toks, width)),
        in_hbm(carry_out.reshape(rows, width)),
        in_hbm(carry_lse),
    )
    return out.reshape(carry_out.shape), lse


def solution(mesh):
    return jax.shard_map(
        functools.partial(body, mesh.shape["ctx"]),
        mesh=mesh,
        in_specs=(
            P("ctx", "kvh", None),
            P(None, "ctx", "kvh", None),
            P("ctx", "kvh", None),
            P("kvh", "ctx"),
        ),
        out_specs=(P("ctx", "kvh", None), P("kvh", "ctx")),
        check_vma=False,
    )
```
